32 devices in a mesh: group: 2 (over y), batch: 4 (over z), mp: 2 (over x), section: 2 (over core).
Axes of the slice: x: 2, y: 2, z: 4, core: 2. Of those that a mesh axis runs over, the one named last changes fastest.
Arguments:
- queries: bfloat16 [2, 192, 8192], P('section', ('group', 'batch'), 'mp'), parts along dimension 1, may hold values from -6 to 6
- new_keys: bfloat16 [2, 192, 1024], P('section', ('group', 'batch'), 'mp'), parts along dimension 1, may hold values from -6 to 6
- new_values: bfloat16 [2, 192, 1024], P('section', ('group', 'batch'), 'mp'), parts along dimension 1, may hold values from -6 to 6
- key_pages: bfloat16 [2, 768, 16, 1024], P('section', ('group', 'batch'), None, 'mp'), parts along dimension 1, may hold values from -6 to 6
- value_pages: bfloat16 [2, 768, 16, 1024], P('section', ('group', 'batch'), None, 'mp'), parts along dimension 1, may hold values from -6 to 6
- page_table: int32 [192, 4], P(('group', 'batch')), parts along dimension 0, may hold values from 0 to 95, as said below
- ancestry: int32 [192], P('group'), parts along dimension 0, may hold values from 0 to 95, as said below
- lengths: int32 [192], P('group'), parts along dimension 0, may hold values from 1 to 64, as said below
- step_rows: bfloat16 [8192, 4096], P(('group', 'batch', 'section'), 'mp'), parts along dimension 0, may hold values from -6 to 6
- norm_gain: float32 [4096], replicated, may hold values from 0.1 to 1.9
- head_weight: bfloat16 [4096, 4096], P(('batch', 'section'), 'mp'), may hold values from -0.09375 to 0.09375
- head_bias: float32 [4096], P('mp'), may hold values from -5 to 5
- class_weight: bfloat16 [4096, 2], P('mp'), may hold values from -0.125 to 0.125
- class_bias: float32 [2], replicated, may hold values from -4 to 4
Outputs:
- attention: bfloat16 [2, 192, 8192], P('section', ('group', 'batch'), 'mp'), parts along dimension 1
- log_odds: float32 [8192], P(('group', 'batch', 'section')), parts along dimension 0
The draws below stay inside these ranges and needn't reach their ends.
There are 2 independent parts, one for each index of `group`. The reference program is written for one: setup_inputs(seed, part) draws one part's arguments, and reference() takes and returns one part's arrays. A program takes and returns all parts, laid end to end along the dimension named above; an argument that names none is the same for every part. Nothing has to cross between parts.
Inputs may be any that keep to these rules, and one draw needn't show every extreme that they name: The pages of the particles on one index of batch lie on that index; the page_table rows of those 24 particles name each of its 96 pages exactly once. Particle j belongs to problem j % 24, and ancestry[j] % 24 == j % 24. Particles j // 24 == d stand on index d of batch; the 24 slots on one index take at most 12 ancestors from any one index, and in every draw some index gives exactly 12 ancestors to the slots of every index. `lengths`: some particle has all 64 positions live in every draw.
All inputs are finite; a program needn't handle non-finite values.
Results may differ from the reference program's by a relative error of at most 0.0043.
Values may be sent and summed in bfloat16 or wider, within the bound.
A program may use at most 64 MiB of HBM per device.

```python
import jax
import jax.numpy as jnp
from jax import lax

QH = 64
KVH = 8
HD = 128
VD = 4096
PAGE = 16
CTX = 64
LAYERS = 2
P_DEV = 24
CAP = 12
PAGES = 4
PARTICLES = 96
POOL = 384
VROWS = 4096


def draw_queries(key, part):
    shape = (LAYERS, PARTICLES, QH, HD)
    base = jnp.clip(jax.random.normal(key, shape, jnp.float32), -6.0, 6.0)
    return base.reshape(LAYERS, PARTICLES, QH * HD).astype(jnp.bfloat16)


def draw_key_pages(key, part):
    shape = (LAYERS, POOL, PAGE, KVH, HD)
    base = jnp.clip(jax.random.normal(key, shape, jnp.float32), -6.0, 6.0)
    return base.reshape(LAYERS, POOL, PAGE, KVH * HD).astype(jnp.bfloat16)


def draw_page_table(key, part):
    device_count = PARTICLES // P_DEV
    per_device = P_DEV * PAGES
    priority = jax.random.randint(key, (device_count, per_device), 0, 65536) * per_device + jnp.arange(per_device)[None, :]
    ordering = jnp.argsort(priority, axis=1)
    return ordering.reshape(PARTICLES, PAGES).astype(jnp.int32)


def draw_ancestry(key, part):
    device_count = PARTICLES // P_DEV
    key_star = jax.random.fold_in(key, 11)
    key_bias = jax.random.fold_in(key, 12)
    noise_random_key = jax.random.fold_in(key, 13)
    key_shuffle = jax.random.fold_in(key, 14)
    star = jax.random.randint(key_star, (), 0, device_count)
    device_bias = jax.random.randint(key_bias, (device_count,), 0, 8)
    noise = jax.random.randint(noise_random_key, (device_count, device_count), 0, 65536)
    device_ids = jnp.arange(device_count)
    priority = (device_bias[None, :] * 65536 + noise) * device_count + device_ids[None, :]
    priority = priority + jnp.where(device_ids == star, 1 << 29, 0)[None, :]
    priority = priority + jnp.where(device_ids[None, :] == device_ids[:, None], 1 << 28, 0)
    ordering = jnp.argsort(-priority, axis=1)
    chosen = ordering[:, jnp.arange(P_DEV) // CAP]
    shuffle_scores = jax.random.randint(key_shuffle, (device_count, P_DEV), 0, 65536) * P_DEV + jnp.arange(P_DEV)[None, :]
    shuffle = jnp.argsort(shuffle_scores, axis=1)
    source = jnp.take_along_axis(chosen, shuffle, axis=1)
    home_position = jnp.argmax((source == device_ids[:, None]).astype(jnp.int32), axis=1)
    last_source = source[:, P_DEV - 1]
    source = source.at[device_ids, home_position].set(last_source)
    source = source.at[:, P_DEV - 1].set(device_ids)
    return (source * P_DEV + jnp.arange(P_DEV)[None, :]).reshape(PARTICLES).astype(jnp.int32)


def draw_lengths(key, part):
    key_values = jax.random.fold_in(key, 21)
    key_longest = jax.random.fold_in(key, 22)
    values = jax.random.randint(key_values, (PARTICLES,), 1, CTX + 1)
    longest = jax.random.randint(key_longest, (), 0, PARTICLES)
    return jnp.where(jnp.arange(PARTICLES) == longest, CTX, values).astype(jnp.int32)


def steps_of(key, shape, shards, least, top_value):
    def one(axis_at, shards_of):
        heights = jax.random.uniform(jax.random.fold_in(jax.random.fold_in(key, 6), axis_at), (shards_of,), jnp.float32, least / len(shards), top_value / len(shards))
        return jnp.repeat(jnp.exp(heights), shape[axis_at] // shards_of).reshape((-1,) + (1,) * (len(shape) - axis_at - 1))

    gain = one(*shards[0])
    for cut in shards[1:]:
        gain = gain * one(*cut)
    return gain


def gaussian(stream_key, extent, spread, limit, shards=(), held_as=jnp.bfloat16):
    values = spread * jax.random.normal(stream_key, extent, jnp.float32)
    if shards:
        values = values * steps_of(stream_key, extent, shards, -0.22, 0.18)
    return jnp.clip(values, -limit, limit).astype(held_as)


def setup_inputs(seed: int = 0, part: int = 0) -> dict:
    key_list = jax.random.split(jax.random.key(seed), 15)
    part_splits = jax.random.split(jax.random.fold_in(key_list[14], part), 15)
    queries = draw_queries(jax.random.fold_in(jax.random.fold_in(key_list[14], part), 71), part)
    new_keys = gaussian(part_splits[1], (LAYERS, PARTICLES, KVH * HD), 1.0, 6.0, ((0, 2), (1, 4), (2, 2)))
    new_values = gaussian(part_splits[2], (LAYERS, PARTICLES, KVH * HD), 1.0, 6.0, ((0, 2), (1, 4), (2, 2)))
    key_pages = draw_key_pages(jax.random.fold_in(jax.random.fold_in(key_list[14], part), 71), part)
    value_pages = gaussian(part_splits[4], (LAYERS, POOL, PAGE, KVH * HD), 1.0, 6.0, ((0, 2), (1, 4), (3, 2)))
    page_table = draw_page_table(jax.random.fold_in(jax.random.fold_in(key_list[14], part), 71), part)
    ancestry = draw_ancestry(jax.random.fold_in(jax.random.fold_in(key_list[14], part), 71), part)
    lengths = draw_lengths(jax.random.fold_in(jax.random.fold_in(key_list[14], part), 71), part)
    step_rows = gaussian(part_splits[8], (VROWS, VD), 1.0, 6.0, ((0, 8), (1, 2)))
    norm_gain = jnp.clip(1.0 + 0.18 * jax.random.normal(key_list[9], (VD,), jnp.float32), 0.1, 1.9)
    head_weight = gaussian(key_list[10], (VD, VD), VD ** -0.5, 0.09375, ((0, 8), (1, 2)))
    head_bias = gaussian(key_list[11], (VD,), 1.0, 5.0, ((0, 2),), jnp.float32)
    class_weight = gaussian(key_list[12], (VD, 2), (VD // 2) ** -0.5, 0.125, ((0, 2),))
    class_bias = gaussian(key_list[13], (2,), 1.0, 4.0, (), jnp.float32)
    return {"queries": queries, "new_keys": new_keys, "new_values": new_values, "key_pages": key_pages, "value_pages": value_pages, "page_table": page_table, "ancestry": ancestry, "lengths": lengths, "step_rows": step_rows, "norm_gain": norm_gain, "head_weight": head_weight, "head_bias": head_bias, "class_weight": class_weight, "class_bias": class_bias}


def reference(queries, new_keys, new_values, key_pages, value_pages, page_table, ancestry, lengths, step_rows, norm_gain, head_weight, head_bias, class_weight, class_bias):
    score_scale = 1.0 / HD ** 0.5
    group_size = QH // KVH
    owner = ancestry // P_DEV
    pool_pages = page_table[ancestry] + (owner * (P_DEV * PAGES))[:, None]
    live_mask = jnp.arange(CTX)[None, :] < lengths[ancestry][:, None]

    def one_layer(layer_args):
        query_per_layer, layer_keys, layer_values, layer_key_pages, layer_value_pages = layer_args
        query_head_count = query_per_layer.reshape(PARTICLES, KVH, group_size, HD).astype(jnp.float32)
        cached_key_rows = layer_key_pages[pool_pages].reshape(PARTICLES, CTX, KVH, HD).astype(jnp.float32)
        cache_values = layer_value_pages[pool_pages].reshape(PARTICLES, CTX, KVH, HD).astype(jnp.float32)
        attention_scores = jnp.einsum('pkgd,ptkd->pkgt', query_head_count, cached_key_rows) * score_scale
        attention_scores = jnp.where(live_mask[:, None, None, :], attention_scores, -1e+30)
        top_score = lax.optimization_barrier(jnp.max(attention_scores, axis=-1))
        weights = jnp.exp(attention_scores - top_score[..., None])
        rounded = lax.optimization_barrier(weights.astype(jnp.bfloat16)).astype(jnp.float32)
        numerator = jnp.einsum('pkgt,ptkd->pkgd', rounded, cache_values)
        particle_key_rows = layer_keys.reshape(PARTICLES, KVH, HD).astype(jnp.float32)
        own_values = layer_values.reshape(PARTICLES, KVH, HD).astype(jnp.float32)
        own_score = jnp.einsum('pkgd,pkd->pkg', query_head_count, particle_key_rows) * score_scale
        own_weight = jnp.exp(own_score - top_score)
        denominator = lax.optimization_barrier(jnp.sum(weights, axis=-1)) + own_weight
        result = (numerator + own_weight[..., None] * own_values[:, :, None, :]) / denominator[..., None]
        return result.reshape(PARTICLES, QH * HD).astype(jnp.bfloat16)
    attention = lax.map(one_layer, (queries, new_keys, new_values, key_pages, value_pages))
    row_values = step_rows.astype(jnp.float32)
    power = lax.optimization_barrier(jnp.mean(row_values * row_values, axis=1, keepdims=True))
    normed = (row_values * lax.rsqrt(power + 1e-06) * norm_gain).astype(jnp.bfloat16)
    hidden = jnp.maximum(jnp.dot(normed, head_weight, preferred_element_type=jnp.float32) + head_bias, 0.0).astype(jnp.bfloat16)
    logits = jnp.dot(hidden, class_weight, preferred_element_type=jnp.float32) + class_bias
    log_odds = logits[:, 1] - logits[:, 0]
    return (attention, log_odds)
```

```python
import functools

import jax
import jax.numpy as jnp
from jax import lax
from jax.experimental import pallas as pl
from jax.experimental.pallas import tpu as pltpu
from jax.sharding import PartitionSpec as P

HD = 128
MESH = pl.DeviceIdType.MESH


def fused_kernel(
    dims,
    table_ref,
    class_bias_ref,
    mail_ref,
    keys_hbm,
    values_hbm,
    rows_hbm,
    gain_ref,
    weight_hbm,
    bias_ref,
    class_ref,
    attention_ref,
    odds_ref,
    mail_in,
    served_out,
    returned,
    keys,
    values,
    raw,
    normed,
    weights,
    total,
    partial,
    logits_in,
    local_sem,
    mail_send,
    mail_recv,
    back_send,
    back_recv,
    line_send,
    line_recv,
    twin_send,
    twin_recv,
    swap_send,
    swap_recv,
    row_send,
    row_recv,
    norm_send,
    norm_recv,
    sum_send,
    sum_recv,
):
    nb, ng, mp, ns = dims["nb"], dims["ng"], dims["mp"], dims["ns"]
    cap, page_count, kvl, group = dims["cap"], dims["page_count"], dims["kvl"], dims["group"]
    half, chunk, chunks, depth = dims["half"], dims["chunk"], dims["chunks"], dims["depth"]
    row_chunks = dims["row_chunks"]
    slots = attention_ref.shape[0]
    heads = kvl * group
    z, y = lax.axis_index("batch"), lax.axis_index("group")
    x, c = lax.axis_index("mp"), lax.axis_index("section")
    other = 1 - c
    twin = 1 - y
    cross = lax.rem(c + y, 2)
    row_count, row_width = rows_hbm.shape
    per_chunk = row_count // row_chunks

    def remote(src, dst, send, recv, device):
        return pltpu.make_async_remote_copy(
            src_ref=src, dst_ref=dst, send_sem=send, recv_sem=recv, device_id=device, device_id_type=MESH
        )

    def columns(owner, n):
        return pl.ds(pl.multiple_of(owner * half + n * chunk, chunk), chunk)

    barrier = pltpu.get_barrier_semaphore()

    def greet(device):
        pl.semaphore_signal(barrier, inc=1, device_id=device, device_id_type=MESH)

    for d in range(1, nb):
        greet({"batch": lax.rem(z + d, nb)})

    @pl.when(z > 0)
    def _():
        greet({"batch": z - 1, "section": other})

    @pl.when(z < nb - 1)
    def _():
        greet({"batch": z + 1, "section": other})

    greet({"section": other})
    greet({"group": twin})
    for d in range(1, mp):
        peer = lax.rem(x + d, mp)
        greet({"mp": peer})
        greet({"mp": peer, "section": other})
    neighbours = jnp.where(z > 0, 1, 0) + jnp.where(z < nb - 1, 1, 0)
    pl.semaphore_wait(barrier, (nb - 1) + 2 + 2 * (mp - 1) + neighbours)

    def mail(d):
        target = lax.rem(z + d, nb)
        return remote(mail_ref.at[target], mail_in.at[z], mail_send.at[d], mail_recv.at[d], {"batch": target})

    def back(d):
        target = lax.rem(z + d, nb)
        return remote(
            served_out.at[target], returned.at[z], back_send.at[d], back_recv.at[d], {"batch": target}
        )

    def row_copy(d, i):
        target = lax.rem(x + d, mp)
        part = pl.ds(i * per_chunk, per_chunk)
        return remote(
            rows_hbm.at[part], raw.at[x, part], row_send.at[d, i], row_recv.at[d, i], {"mp": target}
        )

    def swap(n):
        return remote(
            weight_hbm.at[:, columns(other, n)],
            weights.at[z, c, n],
            swap_send.at[n],
            swap_recv.at[n],
            {"section": other},
        )

    def first_hop(direction, n):
        return remote(
            weight_hbm.at[:, columns(cross, n)],
            weights.at[z, c, n],
            line_send.at[direction, 0, n],
            line_recv.at[direction, 0, n],
            {"batch": z + (1 if direction == 0 else -1), "section": cross},
        )

    def later_hop(direction, hop, n, piece):
        return remote(
            weights.at[piece, cross, n],
            weights.at[piece, cross, n],
            line_send.at[direction, hop, n],
            line_recv.at[direction, hop, n],
            {"batch": z + (1 if direction == 0 else -1)},
        )

    def twin_copy(piece, n, kind):
        return remote(
            weights.at[piece, kind, n],
            weights.at[piece, kind, n],
            twin_send.at[piece, n],
            twin_recv.at[piece, n],
            {"group": twin},
        )

    def norm_copy(i):
        part = pl.ds(i * per_chunk, per_chunk)
        return remote(
            normed.at[c, :, part],
            normed.at[c, :, part],
            norm_send.at[i],
            norm_recv.at[i],
            {"section": other},
        )

    def sum_copy(d, e):
        peer, side = lax.rem(x + d, mp), lax.rem(c + e, 2)
        return remote(
            partial.at[side],
            logits_in.at[d * 2 + e],
            sum_send.at[d * 2 + e],
            sum_recv.at[d * 2 + e],
            {"mp": peer, "section": side},
        )

    own_copies = [
        pltpu.make_async_copy(keys_hbm.at[0], keys, local_sem.at[0]),
        pltpu.make_async_copy(values_hbm.at[0], values, local_sem.at[1]),
        pltpu.make_async_copy(mail_ref.at[z], mail_in.at[z], local_sem.at[2]),
        pltpu.make_async_copy(rows_hbm, raw.at[x], local_sem.at[3]),
    ]
    own_weights = [
        pltpu.make_async_copy(weight_hbm.at[:, columns(c, n)], weights.at[z, c, n], local_sem.at[5 + n])
        for n in range(chunks)
    ]

    for d in range(1, nb):
        mail(d).start()
    for n in range(chunks):

        @pl.when(z < nb - 1)
        def _():
            first_hop(0, n).start()

        @pl.when(z > 0)
        def _():
            first_hop(1, n).start()

    for i in range(row_chunks):
        for d in range(1, mp):
            row_copy(d, i).start()
    for copy in own_copies:
        copy.start()
    for n in range(chunks):
        swap(n).start()
    for copy in own_weights:
        copy.start()

    for side in range(2):
        total[side] = jnp.broadcast_to(
            bias_ref[:, pl.ds(pl.multiple_of(c * half, half), half)], total.shape[1:]
        )

    for copy in own_copies[:3]:
        copy.wait()
    for d in range(1, nb):
        mail(d).wait_recv()

    scale = 1.0 / HD**0.5
    context = page_count * keys.shape[1]
    head_of_row = lax.broadcasted_iota(jnp.int32, (heads, HD), 0) // group
    position = lax.broadcasted_iota(jnp.int32, (heads, context), 1)
    step = 4 if cap % 4 == 0 else cap
    blocks = cap // step

    def serve(d, r):
        base = (d * cap + r) * (page_count + 1)
        pages = [table_ref[base + i] for i in range(page_count)]
        length = table_ref[base + page_count]
        key_block = jnp.concatenate([keys[p] for p in pages], axis=0)
        value_block = jnp.concatenate([values[p] for p in pages], axis=0)
        letter = mail_in[d, r]
        query = letter[:heads]
        own_key = letter[heads : heads + kvl].astype(jnp.float32)
        own_value = letter[heads + kvl : heads + 2 * kvl].astype(jnp.float32)
        zero = jnp.zeros_like(query)
        wide = jnp.concatenate([jnp.where(head_of_row == h, query, zero) for h in range(kvl)], axis=1)
        scores = (
            lax.dot_general(
                wide, key_block, (((1,), (1,)), ((), ())), preferred_element_type=jnp.float32
            )
            * scale
        )
        scores = jnp.where(position < length, scores, -1e30)
        top = jnp.max(scores, axis=1, keepdims=True)
        w = jnp.exp(scores - top)
        den = jnp.sum(w, axis=1, keepdims=True)
        everything = jnp.dot(w.astype(jnp.bfloat16), value_block, preferred_element_type=jnp.float32)
        num = jnp.zeros((heads, HD), jnp.float32)
        key_rows = jnp.zeros((heads, HD), jnp.float32)
        value_rows = jnp.zeros((heads, HD), jnp.float32)
        for h in range(kvl):
            here = head_of_row == h
            num = jnp.where(here, everything[:, h * HD : (h + 1) * HD], num)
            key_rows = jnp.where(here, own_key[h : h + 1], key_rows)
            value_rows = jnp.where(here, own_value[h : h + 1], value_rows)
        own_score = jnp.sum(query.astype(jnp.float32) * key_rows, axis=1, keepdims=True) * scale
        own = jnp.exp(own_score - top)
        return ((num + own * value_rows) / (den + own)).astype(jnp.bfloat16)

    def serve_block(index, carry):
        d, r0 = index // blocks, lax.rem(index, blocks) * step
        results = [serve(d, r0 + u) for u in range(step)]
        for u in range(step):
            served_out[d, r0 + u] = results[u]
        return carry

    lax.fori_loop(0, nb * blocks, serve_block, 0)
    for d in range(1, nb):
        back(d).start()
    own_back = pltpu.make_async_copy(served_out.at[z], returned.at[z], local_sem.at[4])
    own_back.start()

    def line_step(r, n):
        @pl.when(z - r >= 0)
        def _():
            piece = z - r
            later_hop(0, r - 1, n, piece).wait_recv()

            @pl.when(z + 1 < nb)
            def _():
                later_hop(0, r, n, piece).start()

            twin_copy(piece, n, cross).start()

        @pl.when(z + r < nb)
        def _():
            piece = z + r
            later_hop(1, r - 1, n, piece).wait_recv()

            @pl.when(z > 0)
            def _():
                later_hop(1, r, n, piece).start()

            twin_copy(piece, n, cross).start()

    features = row_width * mp
    pieces_per_block = row_width // depth
    fine = min(16, per_chunk)

    def row_step(i):
        for d in range(1, mp):
            row_copy(d, i).wait_recv()

        def normalise(j, carry):
            start = pl.multiple_of(i * per_chunk + j * fine, fine)
            part = pl.ds(start, fine)
            power = jnp.zeros((fine, 1), jnp.float32)
            for b in range(mp):
                block = raw[b, part].astype(jnp.float32)
                power = power + jnp.sum(block * block, axis=1, keepdims=True)
            factor = lax.rsqrt(power / features + 1e-06)
            for b in range(mp):
                block = raw[b, part].astype(jnp.float32)
                gain = gain_ref[:, b * row_width : (b + 1) * row_width]
                result = (block * factor * gain).astype(jnp.bfloat16)
                for p in range(pieces_per_block):
                    normed[c, b * pieces_per_block + p, part] = result[:, p * depth : (p + 1) * depth]
            return carry

        lax.fori_loop(0, per_chunk // fine, normalise, 0)
        norm_copy(i).start()

    own_copies[3].wait()
    early = [(r, n) for r in range(1, nb - 1) for n in range(chunks)]
    for i in range(row_chunks):
        for r, n in early[len(early) * i // row_chunks : len(early) * (i + 1) // row_chunks]:
            line_step(r, n)
        row_step(i)
    for i in range(row_chunks):
        norm_copy(i).wait_recv()

    def multiply(piece, kind, n):
        for side in range(2):
            total[side, :, n * chunk : (n + 1) * chunk] += jnp.dot(
                normed[side, piece * ns + kind], weights[piece, kind, n], preferred_element_type=jnp.float32
            )

    def multiply_own(n):
        own_weights[n].wait()
        swap(n).wait_recv()
        multiply(z, 0, n)
        multiply(z, 1, n)

    def multiply_at(r, n):
        def both(piece):
            multiply(piece, cross, n)
            twin_copy(piece, n, 1 - cross).wait_recv()
            multiply(piece, 1 - cross, n)

        def left():
            both(z - r)

        def right():
            both(z + r)

        pl.when(z - r >= 0)(left)
        pl.when(z + r < nb)(right)

    for n in range(chunks):
        multiply_own(n)

        def near(r, carry):
            multiply_at(r, n)
            return carry

        lax.fori_loop(1, nb - 1, near, 0)
        line_step(nb - 1, n)

    for n in range(chunks):
        multiply_at(nb - 1, n)

    class_part = class_ref[:, pl.ds(pl.multiple_of(c * half, half), half)]
    for side in range(2):
        hidden = jnp.maximum(total[side], 0.0).astype(jnp.bfloat16)
        partial[side] = lax.dot_general(
            class_part, hidden, (((1,), (1,)), ((), ())), preferred_element_type=jnp.float32
        )
    pairs = [(d, e) for d in range(mp) for e in range(2) if d or e]
    for d, e in pairs:
        sum_copy(d, e).start()

    own_back.wait()
    for d in range(1, nb):
        back(d).wait_recv()
    pick = nb * cap * (page_count + 1)

    def place(j, carry):
        attention_ref[j] = returned[table_ref[pick + j], table_ref[pick + slots + j]]
        return carry

    lax.fori_loop(0, slots, place, 0)

    logits = partial[c]
    for d, e in pairs:
        sum_copy(d, e).wait_recv()
        logits = logits + logits_in[d * 2 + e]
    odds_ref[...] = (logits[1:2] + class_bias_ref[1]) - (logits[0:1] + class_bias_ref[0])

    for d in range(1, nb):
        mail(d).wait_send()
        back(d).wait_send()
    for i in range(row_chunks):
        for d in range(1, mp):
            row_copy(d, i).wait_send()
        norm_copy(i).wait_send()
    for d, e in pairs:
        sum_copy(d, e).wait_send()
    for n in range(chunks):
        swap(n).wait_send()

        @pl.when(z < nb - 1)
        def _():
            first_hop(0, n).wait_send()

        @pl.when(z > 0)
        def _():
            first_hop(1, n).wait_send()

        def drain(r, carry):
            @pl.when(z - r >= 0)
            def _():
                @pl.when(z + 1 < nb)
                def _():
                    later_hop(0, r, n, z - r).wait_send()

                twin_copy(z - r, n, cross).wait_send()

            @pl.when(z + r < nb)
            def _():
                @pl.when(z > 0)
                def _():
                    later_hop(1, r, n, z + r).wait_send()

                twin_copy(z + r, n, cross).wait_send()

            return carry

        lax.fori_loop(1, nb, drain, 0)


def per_device(
    queries,
    new_keys,
    new_values,
    key_pages,
    value_pages,
    page_table,
    ancestry,
    lengths,
    step_rows,
    norm_gain,
    head_weight,
    head_bias,
    class_weight,
    class_bias,
):
    slot_count, page_count = page_table.shape
    kv_width = key_pages.shape[3]
    kvl = kv_width // HD
    group = queries.shape[2] // kv_width
    heads = kvl * group
    nb, ng = lax.axis_size("batch"), lax.axis_size("group")
    mp, ns = lax.axis_size("mp"), lax.axis_size("section")
    assert ng == 2 and ns == 2 and queries.shape[0] == 1
    z = lax.axis_index("batch")
    cap = max(2, (2 * slot_count + nb - 1) // nb)

    source = (ancestry // slot_count).reshape(nb, slot_count)
    positions = jnp.arange(slot_count)
    earlier = positions[None, :] < positions[:, None]
    same_source = source[:, :, None] == source[:, None, :]
    rank = jnp.sum(same_source & earlier[None, :, :], axis=2)
    slot_ids = jnp.arange(cap)
    served = (source == z)[:, None, :] & (rank[:, None, :] == slot_ids[None, :, None])
    served_slot = jnp.sum(jnp.where(served, positions[None, None, :], 0), axis=2)
    own_source = lax.dynamic_index_in_dim(source, z, 0, keepdims=False)
    own_rank = lax.dynamic_index_in_dim(rank, z, 0, keepdims=False)
    local_lengths = lax.dynamic_slice_in_dim(lengths, z * slot_count, slot_count)
    facts = jnp.concatenate([page_table, local_lengths[:, None]], axis=1)
    table = jnp.concatenate([facts[served_slot].reshape(-1), own_source, own_rank])
    wanted = (own_source[None, None, :] == jnp.arange(nb)[:, None, None]) & (
        own_rank[None, None, :] == slot_ids[None, :, None]
    )
    request_slot = jnp.sum(jnp.where(wanted, positions[None, None, :], 0), axis=2)
    letters = jnp.concatenate([queries[0], new_keys[0], new_values[0]], axis=1)
    lines = heads + 2 * kvl
    mail = jnp.take(letters, request_slot.reshape(-1), axis=0).reshape(nb, cap, lines, HD)

    row_count, row_width = step_rows.shape
    depth, width = head_weight.shape
    half = width // ns
    chunk = min(256, half)
    chunks = half // chunk
    row_chunks = 4
    pieces = nb * ns
    dims = dict(
        nb=nb, ng=ng, mp=mp, ns=ns, cap=cap, page_count=page_count, kvl=kvl, group=group,
        half=half, chunk=chunk, chunks=chunks, depth=depth, row_chunks=row_chunks,
    )
    class_rows = jnp.zeros((8, width), class_weight.dtype).at[:2].set(class_weight.T)
    smem = pl.BlockSpec(memory_space=pltpu.SMEM)
    vmem = pl.BlockSpec(memory_space=pltpu.VMEM)
    anywhere = pl.BlockSpec(memory_space=pl.ANY)
    bf16, f32 = jnp.bfloat16, jnp.float32
    sems = pltpu.SemaphoreType.DMA
    attention, odds = pl.pallas_call(
        functools.partial(fused_kernel, dims),
        out_shape=(
            jax.ShapeDtypeStruct((slot_count, heads, HD), bf16),
            jax.ShapeDtypeStruct((1, row_count), f32),
        ),
        in_specs=[smem, smem, vmem, anywhere, anywhere, anywhere, vmem, anywhere, vmem, vmem],
        out_specs=(vmem, vmem),
        scratch_shapes=[
            pltpu.VMEM((nb, cap, lines, HD), bf16),
            pltpu.VMEM((nb, cap, heads, HD), bf16),
            pltpu.VMEM((nb, cap, heads, HD), bf16),
            pltpu.VMEM(key_pages.shape[1:], bf16),
            pltpu.VMEM(key_pages.shape[1:], bf16),
            pltpu.VMEM((mp, row_count, row_width), bf16),
            pltpu.VMEM((2, pieces, row_count, depth), bf16),
            pltpu.VMEM((nb, ns, chunks, depth, chunk), bf16),
            pltpu.VMEM((2, row_count, half), f32),
            pltpu.VMEM((2, 8, row_count), f32),
            pltpu.VMEM((2 * mp, 8, row_count), f32),
            sems((5 + chunks,)),
            sems((nb,)),
            sems((nb,)),
            sems((nb,)),
            sems((nb,)),
            sems((2, nb, chunks)),
            sems((2, nb, chunks)),
            sems((nb, chunks)),
            sems((nb, chunks)),
            sems((chunks,)),
            sems((chunks,)),
            sems((mp, row_chunks)),
            sems((mp, row_chunks)),
            sems((row_chunks,)),
            sems((row_chunks,)),
            sems((2 * mp,)),
            sems((2 * mp,)),
        ],
        compiler_params=pltpu.CompilerParams(
            collective_id=0, has_side_effects=True, vmem_limit_bytes=60 * 1024 * 1024
        ),
        name="filter_round",
    )(
        table,
        class_bias,
        mail,
        key_pages,
        value_pages,
        step_rows,
        norm_gain.reshape(1, -1),
        head_weight,
        head_bias.reshape(1, -1),
        class_rows,
    )
    return attention.reshape(1, slot_count, heads * HD), odds.reshape(-1)


def solution(mesh):
    placed = (
        P("section", ("group", "batch"), "mp"),
        P("section", ("group", "batch"), "mp"),
        P("section", ("group", "batch"), "mp"),
        P("section", ("group", "batch"), None, "mp"),
        P("section", ("group", "batch"), None, "mp"),
        P(("group", "batch"), None),
        P("group"),
        P("group"),
        P(("group", "batch", "section"), "mp"),
        P(),
        P(("batch", "section"), "mp"),
        P("mp"),
        P("mp", None),
        P(),
    )
    return jax.shard_map(
        per_device,
        mesh=mesh,
        in_specs=placed,
        out_specs=(P("section", ("group", "batch"), "mp"), P(("group", "batch", "section"))),
        check_vma=False,
    )
```

```python
import functools

import jax
import jax.numpy as jnp
from jax import lax
from jax.experimental import pallas as pl
from jax.experimental.pallas import tpu as pltpu
from jax.sharding import PartitionSpec as P

HD = 128
MESH = pl.DeviceIdType.MESH


def fused_kernel(
    dims,
    table_ref,
    class_bias_ref,
    mail_ref,
    keys_hbm,
    values_hbm,
    rows_hbm,
    gain_ref,
    weight_hbm,
    bias_ref,
    class_ref,
    attention_ref,
    odds_ref,
    mail_in,
    served_out,
    returned,
    keys,
    values,
    raw,
    normed,
    weights,
    total,
    partial,
    logits_in,
    gathered,
    local_sem,
    mail_send,
    mail_recv,
    back_send,
    back_recv,
    line_send,
    line_recv,
    twin_send,
    twin_recv,
    swap_send,
    swap_recv,
    row_send,
    row_recv,
    norm_send,
    norm_recv,
    sum_send,
    sum_recv,
):
    nb, ng, mp, ns = dims["nb"], dims["ng"], dims["mp"], dims["ns"]
    cap, page_count, kvl, group = dims["cap"], dims["page_count"], dims["kvl"], dims["group"]
    half, chunk, chunks, depth = dims["half"], dims["chunk"], dims["chunks"], dims["depth"]
    row_chunks = dims["row_chunks"]
    slots = attention_ref.shape[0]
    heads = kvl * group
    z, y = lax.axis_index("batch"), lax.axis_index("group")
    x, c = lax.axis_index("mp"), lax.axis_index("section")
    other = 1 - c
    twin = 1 - y
    cross = lax.rem(c + y, 2)
    row_count, row_width = rows_hbm.shape
    per_chunk = row_count // row_chunks

    def remote(src, dst, send, recv, device):
        return pltpu.make_async_remote_copy(
            src_ref=src, dst_ref=dst, send_sem=send, recv_sem=recv, device_id=device, device_id_type=MESH
        )

    def columns(owner, n):
        return pl.ds(pl.multiple_of(owner * half + n * chunk, chunk), chunk)

    barrier = pltpu.get_barrier_semaphore()

    def greet(device):
        pl.semaphore_signal(barrier, inc=1, device_id=device, device_id_type=MESH)

    for d in range(1, nb):
        greet({"batch": lax.rem(z + d, nb)})

    @pl.when(z > 0)
    def _():
        greet({"batch": z - 1, "section": other})

    @pl.when(z < nb - 1)
    def _():
        greet({"batch": z + 1, "section": other})

    greet({"section": other})
    greet({"group": twin})
    for d in range(1, mp):
        peer = lax.rem(x + d, mp)
        greet({"mp": peer})
        greet({"mp": peer, "section": other})
    neighbours = jnp.where(z > 0, 1, 0) + jnp.where(z < nb - 1, 1, 0)
    pl.semaphore_wait(barrier, (nb - 1) + 2 + 2 * (mp - 1) + neighbours)

    def mail(d):
        target = lax.rem(z + d, nb)
        return remote(mail_ref.at[target], mail_in.at[z], mail_send.at[d], mail_recv.at[d], {"batch": target})

    def back(d):
        target = lax.rem(z + d, nb)
        return remote(
            served_out.at[target], returned.at[z], back_send.at[d], back_recv.at[d], {"batch": target}
        )

    def row_copy(d, i):
        target = lax.rem(x + d, mp)
        part = pl.ds(i * per_chunk, per_chunk)
        return remote(
            rows_hbm.at[part], raw.at[x, part], row_send.at[d, i], row_recv.at[d, i], {"mp": target}
        )

    def swap(n):
        return remote(
            weight_hbm.at[:, columns(other, n)],
            weights.at[z, c, n],
            swap_send.at[n],
            swap_recv.at[n],
            {"section": other},
        )

    parts = 2 * chunks
    sub = depth // 2

    def lines(q):
        return pl.ds((q % 2) * sub, sub)

    def first_hop(direction, q):
        return remote(
            weight_hbm.at[lines(q), columns(cross, q // 2)],
            weights.at[z, c, q // 2, lines(q)],
            line_send.at[direction, 0, q],
            line_recv.at[direction, 0, q],
            {"batch": z + (1 if direction == 0 else -1), "section": cross},
        )

    def later_hop(direction, hop, q, piece):
        return remote(
            weights.at[piece, cross, q // 2, lines(q)],
            weights.at[piece, cross, q // 2, lines(q)],
            line_send.at[direction, hop, q],
            line_recv.at[direction, hop, q],
            {"batch": z + (1 if direction == 0 else -1)},
        )

    def twin_copy(piece, q, kind):
        return remote(
            weights.at[piece, kind, q // 2, lines(q)],
            weights.at[piece, kind, q // 2, lines(q)],
            twin_send.at[piece, q],
            twin_recv.at[piece, q],
            {"group": twin},
        )

    def norm_copy(i):
        part = pl.ds(i * per_chunk, per_chunk)
        return remote(
            normed.at[c, :, part],
            normed.at[c, :, part],
            norm_send.at[i],
            norm_recv.at[i],
            {"section": other},
        )

    def sum_copy(d, e):
        peer, side = lax.rem(x + d, mp), lax.rem(c + e, 2)
        return remote(
            partial.at[side],
            logits_in.at[d * 2 + e],
            sum_send.at[d * 2 + e],
            sum_recv.at[d * 2 + e],
            {"mp": peer, "section": side},
        )

    own_copies = [
        pltpu.make_async_copy(keys_hbm.at[0], keys, local_sem.at[0]),
        pltpu.make_async_copy(values_hbm.at[0], values, local_sem.at[1]),
        pltpu.make_async_copy(mail_ref.at[z], mail_in.at[z], local_sem.at[2]),
        pltpu.make_async_copy(rows_hbm, raw.at[x], local_sem.at[3]),
    ]
    own_weights = [
        pltpu.make_async_copy(weight_hbm.at[:, columns(c, n)], weights.at[z, c, n], local_sem.at[5 + n])
        for n in range(chunks)
    ]

    for d in range(1, nb):
        mail(d).start()
    for q in range(parts):

        @pl.when(z < nb - 1)
        def _():
            first_hop(0, q).start()

        @pl.when(z > 0)
        def _():
            first_hop(1, q).start()

    for i in range(row_chunks):
        for d in range(1, mp):
            row_copy(d, i).start()
    for copy in own_copies:
        copy.start()
    for n in range(chunks):
        swap(n).start()
    for copy in own_weights:
        copy.start()

    for side in range(2):
        total[side] = jnp.broadcast_to(
            bias_ref[:, pl.ds(pl.multiple_of(c * half, half), half)], total.shape[1:]
        )

    for copy in own_copies[:3]:
        copy.wait()
    for d in range(1, nb):
        mail(d).wait_recv()

    scale = 1.0 / HD**0.5
    context = page_count * keys.shape[1]
    head_of_row = lax.broadcasted_iota(jnp.int32, (heads, HD), 0) // group
    position = lax.broadcasted_iota(jnp.int32, (heads, context), 1)
    step = 4 if cap % 4 == 0 else cap
    blocks = cap // step

    def serve(d, r):
        base = (d * cap + r) * (page_count + 1)
        pages = [table_ref[base + i] for i in range(page_count)]
        length = table_ref[base + page_count]
        key_block = jnp.concatenate([keys[p] for p in pages], axis=0)
        value_block = jnp.concatenate([values[p] for p in pages], axis=0)
        letter = mail_in[d, r]
        query = letter[:heads]
        own_key = letter[heads : heads + kvl].astype(jnp.float32)
        own_value = letter[heads + kvl : heads + 2 * kvl].astype(jnp.float32)
        zero = jnp.zeros_like(query)
        wide = jnp.concatenate([jnp.where(head_of_row == h, query, zero) for h in range(kvl)], axis=1)
        scores = (
            lax.dot_general(
                wide, key_block, (((1,), (1,)), ((), ())), preferred_element_type=jnp.float32
            )
            * scale
        )
        scores = jnp.where(position < length, scores, -1e30)
        top = jnp.max(scores, axis=1, keepdims=True)
        w = jnp.exp(scores - top)
        den = jnp.sum(w, axis=1, keepdims=True)
        everything = jnp.dot(w.astype(jnp.bfloat16), value_block, preferred_element_type=jnp.float32)
        num = jnp.zeros((heads, HD), jnp.float32)
        key_rows = jnp.zeros((heads, HD), jnp.float32)
        value_rows = jnp.zeros((heads, HD), jnp.float32)
        for h in range(kvl):
            here = head_of_row == h
            num = jnp.where(here, everything[:, h * HD : (h + 1) * HD], num)
            key_rows = jnp.where(here, own_key[h : h + 1], key_rows)
            value_rows = jnp.where(here, own_value[h : h + 1], value_rows)
        own_score = jnp.sum(query.astype(jnp.float32) * key_rows, axis=1, keepdims=True) * scale
        own = jnp.exp(own_score - top)
        return ((num + own * value_rows) / (den + own)).astype(jnp.bfloat16)

    def serve_block(index, carry):
        d, r0 = index // blocks, lax.rem(index, blocks) * step
        results = [serve(d, r0 + u) for u in range(step)]
        for u in range(step):
            served_out[d, r0 + u] = results[u]
        return carry

    lax.fori_loop(0, nb * blocks, serve_block, 0)
    for d in range(1, nb):
        back(d).start()
    own_back = pltpu.make_async_copy(served_out.at[z], returned.at[z], local_sem.at[4])
    own_back.start()

    def line_step(r, q):
        @pl.when(z - r >= 0)
        def _():
            piece = z - r
            later_hop(0, r - 1, q, piece).wait_recv()

            @pl.when(z + 1 < nb)
            def _():
                later_hop(0, r, q, piece).start()

            twin_copy(piece, q, cross).start()

        @pl.when(z + r < nb)
        def _():
            piece = z + r
            later_hop(1, r - 1, q, piece).wait_recv()

            @pl.when(z > 0)
            def _():
                later_hop(1, r, q, piece).start()

            twin_copy(piece, q, cross).start()

    features = row_width * mp
    pieces_per_block = row_width // depth
    fine = min(16, per_chunk)

    def row_step(i):
        for d in range(1, mp):
            row_copy(d, i).wait_recv()

        def normalise(j, carry):
            start = pl.multiple_of(i * per_chunk + j * fine, fine)
            part = pl.ds(start, fine)
            power = jnp.zeros((fine, 1), jnp.float32)
            for b in range(mp):
                block = raw[b, part].astype(jnp.float32)
                power = power + jnp.sum(block * block, axis=1, keepdims=True)
            factor = lax.rsqrt(power / features + 1e-06)
            for b in range(mp):
                block = raw[b, part].astype(jnp.float32)
                gain = gain_ref[:, b * row_width : (b + 1) * row_width]
                result = (block * factor * gain).astype(jnp.bfloat16)
                for p in range(pieces_per_block):
                    normed[c, b * pieces_per_block + p, part] = result[:, p * depth : (p + 1) * depth]
            return carry

        lax.fori_loop(0, per_chunk // fine, normalise, 0)
        norm_copy(i).start()

    own_copies[3].wait()
    early = [(r, q) for r in range(1, nb - 1) for q in range(parts)]
    for i in range(row_chunks):
        for r, q in early[len(early) * i // row_chunks : len(early) * (i + 1) // row_chunks]:
            line_step(r, q)
        row_step(i)
    for i in range(row_chunks):
        norm_copy(i).wait_recv()

    def multiply(piece, kind, n):
        for side in range(2):
            total[side, :, n * chunk : (n + 1) * chunk] += jnp.dot(
                normed[side, piece * ns + kind], weights[piece, kind, n], preferred_element_type=jnp.float32
            )

    def multiply_own(n):
        own_weights[n].wait()
        swap(n).wait_recv()
        multiply(z, 0, n)
        multiply(z, 1, n)

    def multiply_at(r, n):
        def both(piece):
            multiply(piece, cross, n)
            twin_copy(piece, 2 * n, 1 - cross).wait_recv()
            twin_copy(piece, 2 * n + 1, 1 - cross).wait_recv()
            multiply(piece, 1 - cross, n)

        def left():
            both(z - r)

        def right():
            both(z + r)

        pl.when(z - r >= 0)(left)
        pl.when(z + r < nb)(right)

    def place_attention():
        own_back.wait()
        for d in range(1, nb):
            back(d).wait_recv()
        pick = nb * cap * (page_count + 1)

        def place(j, carry):
            gathered[j] = returned[table_ref[pick + j], table_ref[pick + slots + j]].astype(jnp.float32)
            return carry

        lax.fori_loop(0, slots, place, 0)
        for h in range(heads):
            attention_ref[:, h * HD : (h + 1) * HD] = gathered[:, h, :].astype(jnp.bfloat16)

    for n in range(chunks):
        multiply_own(n)

        def near(r, carry):
            multiply_at(r, n)
            return carry

        lax.fori_loop(1, nb - 1, near, 0)
        line_step(nb - 1, 2 * n)
        line_step(nb - 1, 2 * n + 1)
        if n > 0:
            multiply_at(nb - 1, n - 1)
        if n == chunks - 2:
            place_attention()

    if chunks == 1:
        place_attention()
    multiply_at(nb - 1, chunks - 1)

    class_part = class_ref[:, pl.ds(pl.multiple_of(c * half, half), half)]
    for side in range(2):
        hidden = jnp.maximum(total[side], 0.0).astype(jnp.bfloat16)
        partial[side] = lax.dot_general(
            class_part, hidden, (((1,), (1,)), ((), ())), preferred_element_type=jnp.float32
        )
    pairs = [(d, e) for d in range(mp) for e in range(2) if d or e]
    for d, e in pairs:
        sum_copy(d, e).start()

    logits = partial[c]
    for d, e in pairs:
        sum_copy(d, e).wait_recv()
        logits = logits + logits_in[d * 2 + e]
    odds_ref[...] = (logits[1:2] + class_bias_ref[1]) - (logits[0:1] + class_bias_ref[0])

    for d in range(1, nb):
        mail(d).wait_send()
        back(d).wait_send()
    for i in range(row_chunks):
        for d in range(1, mp):
            row_copy(d, i).wait_send()
        norm_copy(i).wait_send()
    for d, e in pairs:
        sum_copy(d, e).wait_send()
    for n in range(chunks):
        swap(n).wait_send()
    for q in range(parts):

        @pl.when(z < nb - 1)
        def _():
            first_hop(0, q).wait_send()

        @pl.when(z > 0)
        def _():
            first_hop(1, q).wait_send()

        def drain(r, carry):
            @pl.when(z - r >= 0)
            def _():
                @pl.when(z + 1 < nb)
                def _():
                    later_hop(0, r, q, z - r).wait_send()

                twin_copy(z - r, q, cross).wait_send()

            @pl.when(z + r < nb)
            def _():
                @pl.when(z > 0)
                def _():
                    later_hop(1, r, q, z + r).wait_send()

                twin_copy(z + r, q, cross).wait_send()

            return carry

        lax.fori_loop(1, nb, drain, 0)


def per_device(
    queries,
    new_keys,
    new_values,
    key_pages,
    value_pages,
    page_table,
    ancestry,
    lengths,
    step_rows,
    norm_gain,
    head_weight,
    head_bias,
    class_weight,
    class_bias,
):
    slot_count, page_count = page_table.shape
    kv_width = key_pages.shape[3]
    kvl = kv_width // HD
    group = queries.shape[2] // kv_width
    heads = kvl * group
    nb, ng = lax.axis_size("batch"), lax.axis_size("group")
    mp, ns = lax.axis_size("mp"), lax.axis_size("section")
    assert ng == 2 and ns == 2 and queries.shape[0] == 1
    z = lax.axis_index("batch")
    cap = max(2, (2 * slot_count + nb - 1) // nb)

    source = (ancestry // slot_count).reshape(nb, slot_count)
    positions = jnp.arange(slot_count)
    earlier = positions[None, :] < positions[:, None]
    same_source = source[:, :, None] == source[:, None, :]
    rank = jnp.sum(same_source & earlier[None, :, :], axis=2)
    slot_ids = jnp.arange(cap)
    served = (source == z)[:, None, :] & (rank[:, None, :] == slot_ids[None, :, None])
    served_slot = jnp.sum(jnp.where(served, positions[None, None, :], 0), axis=2)
    own_source = lax.dynamic_index_in_dim(source, z, 0, keepdims=False)
    own_rank = lax.dynamic_index_in_dim(rank, z, 0, keepdims=False)
    local_lengths = lax.dynamic_slice_in_dim(lengths, z * slot_count, slot_count)
    facts = jnp.concatenate([page_table, local_lengths[:, None]], axis=1)
    table = jnp.concatenate([facts.at[served_slot.reshape(-1)].get(mode="promise_in_bounds").reshape(-1), own_source, own_rank])
    wanted = (own_source[None, None, :] == jnp.arange(nb)[:, None, None]) & (
        own_rank[None, None, :] == slot_ids[None, :, None]
    )
    request_slot = jnp.sum(jnp.where(wanted, positions[None, None, :], 0), axis=2)
    letters = jnp.concatenate([queries[0], new_keys[0], new_values[0]], axis=1)
    lines = heads + 2 * kvl
    mail = letters.at[request_slot.reshape(-1)].get(mode="promise_in_bounds").reshape(nb, cap, lines, HD)

    row_count, row_width = step_rows.shape
    depth, width = head_weight.shape
    half = width // ns
    chunk = min(256, half)
    chunks = half // chunk
    row_chunks = 4
    pieces = nb * ns
    dims = dict(
        nb=nb, ng=ng, mp=mp, ns=ns, cap=cap, page_count=page_count, kvl=kvl, group=group,
        half=half, chunk=chunk, chunks=chunks, depth=depth, row_chunks=row_chunks,
    )
    class_rows = jnp.zeros((8, width), class_weight.dtype).at[:2].set(class_weight.T)
    smem = pl.BlockSpec(memory_space=pltpu.SMEM)
    vmem = pl.BlockSpec(memory_space=pltpu.VMEM)
    anywhere = pl.BlockSpec(memory_space=pl.ANY)
    bf16, f32 = jnp.bfloat16, jnp.float32
    sems = pltpu.SemaphoreType.DMA
    attention, odds = pl.pallas_call(
        functools.partial(fused_kernel, dims),
        out_shape=(
            jax.ShapeDtypeStruct((slot_count, heads * HD), bf16),
            jax.ShapeDtypeStruct((1, row_count), f32),
        ),
        in_specs=[smem, smem, vmem, anywhere, anywhere, anywhere, vmem, anywhere, vmem, vmem],
        out_specs=(vmem, vmem),
        scratch_shapes=[
            pltpu.VMEM((nb, cap, lines, HD), bf16),
            pltpu.VMEM((nb, cap, heads, HD), bf16),
            pltpu.VMEM((nb, cap, heads, HD), bf16),
            pltpu.VMEM(key_pages.shape[1:], bf16),
            pltpu.VMEM(key_pages.shape[1:], bf16),
            pltpu.VMEM((mp, row_count, row_width), bf16),
            pltpu.VMEM((2, pieces, row_count, depth), bf16),
            pltpu.VMEM((nb, ns, chunks, depth, chunk), bf16),
            pltpu.VMEM((2, row_count, half), f32),
            pltpu.VMEM((2, 8, row_count), f32),
            pltpu.VMEM((2 * mp, 8, row_count), f32),
            pltpu.VMEM((slot_count, heads, HD), f32),
            sems((5 + chunks,)),
            sems((nb,)),
            sems((nb,)),
            sems((nb,)),
            sems((nb,)),
            sems((2, nb, 2 * chunks)),
            sems((2, nb, 2 * chunks)),
            sems((nb, 2 * chunks)),
            sems((nb, 2 * chunks)),
            sems((chunks,)),
            sems((chunks,)),
            sems((mp, row_chunks)),
            sems((mp, row_chunks)),
            sems((row_chunks,)),
            sems((row_chunks,)),
            sems((2 * mp,)),
            sems((2 * mp,)),
        ],
        compiler_params=pltpu.CompilerParams(
            collective_id=0, has_side_effects=True, vmem_limit_bytes=60 * 1024 * 1024
        ),
        name="filter_round",
    )(
        table,
        class_bias,
        mail,
        key_pages,
        value_pages,
        step_rows,
        norm_gain.reshape(1, -1),
        head_weight,
        head_bias.reshape(1, -1),
        class_rows,
    )
    return attention[None], odds.reshape(-1)


def solution(mesh):
    placed = (
        P("section", ("group", "batch"), "mp"),
        P("section", ("group", "batch"), "mp"),
        P("section", ("group", "batch"), "mp"),
        P("section", ("group", "batch"), None, "mp"),
        P("section", ("group", "batch"), None, "mp"),
        P(("group", "batch"), None),
        P("group"),
        P("group"),
        P(("group", "batch", "section"), "mp"),
        P(),
        P(("batch", "section"), "mp"),
        P("mp"),
        P("mp", None),
        P(),
    )
    return jax.shard_map(
        per_device,
        mesh=mesh,
        in_specs=placed,
        out_specs=(P("section", ("group", "batch"), "mp"), P(("group", "batch", "section"))),
        check_vma=False,
    )
```

```python
import functools

import jax
import jax.numpy as jnp
from jax import lax
from jax.experimental import pallas as pl
from jax.experimental.pallas import tpu as pltpu
from jax.sharding import PartitionSpec as P

HD = 128
MESH = pl.DeviceIdType.MESH


def fused_kernel(
    dims,
    table_ref,
    class_bias_ref,
    mail_ref,
    keys_hbm,
    values_hbm,
    rows_hbm,
    gain_ref,
    weight_hbm,
    bias_ref,
    class_ref,
    attention_ref,
    odds_ref,
    mail_in,
    served_out,
    returned,
    keys,
    values,
    raw,
    normed,
    weights,
    total,
    partial,
    logits_in,
    local_sem,
    mail_send,
    mail_recv,
    back_send,
    back_recv,
    line_send,
    line_recv,
    twin_send,
    twin_recv,
    swap_send,
    swap_recv,
    row_send,
    row_recv,
    norm_send,
    norm_recv,
    sum_send,
    sum_recv,
):
    nb, ng, mp, ns = dims["nb"], dims["ng"], dims["mp"], dims["ns"]
    cap, page_count, kvl, group = dims["cap"], dims["page_count"], dims["kvl"], dims["group"]
    half, chunk, chunks, depth = dims["half"], dims["chunk"], dims["chunks"], dims["depth"]
    row_chunks = dims["row_chunks"]
    slots = attention_ref.shape[0]
    heads = kvl * group
    z, y = lax.axis_index("batch"), lax.axis_index("group")
    x, c = lax.axis_index("mp"), lax.axis_index("section")
    other = 1 - c
    twin = 1 - y
    cross = lax.rem(c + y, 2)
    row_count, row_width = rows_hbm.shape
    per_chunk = row_count // row_chunks

    def remote(src, dst, send, recv, device):
        return pltpu.make_async_remote_copy(
            src_ref=src, dst_ref=dst, send_sem=send, recv_sem=recv, device_id=device, device_id_type=MESH
        )

    def columns(owner, n):
        return pl.ds(pl.multiple_of(owner * half + n * chunk, chunk), chunk)

    barrier = pltpu.get_barrier_semaphore()

    def greet(device):
        pl.semaphore_signal(barrier, inc=1, device_id=device, device_id_type=MESH)

    for d in range(1, nb):
        greet({"batch": lax.rem(z + d, nb)})

    @pl.when(z > 0)
    def _():
        greet({"batch": z - 1, "section": other})

    @pl.when(z < nb - 1)
    def _():
        greet({"batch": z + 1, "section": other})

    greet({"section": other})
    greet({"group": twin})
    for d in range(1, mp):
        peer = lax.rem(x + d, mp)
        greet({"mp": peer})
        greet({"mp": peer, "section": other})
    neighbours = jnp.where(z > 0, 1, 0) + jnp.where(z < nb - 1, 1, 0)
    pl.semaphore_wait(barrier, (nb - 1) + 2 + 2 * (mp - 1) + neighbours)

    def mail(d):
        target = lax.rem(z + d, nb)
        return remote(mail_ref.at[target], mail_in.at[z], mail_send.at[d], mail_recv.at[d], {"batch": target})

    def back(d):
        target = lax.rem(z + d, nb)
        return remote(
            served_out.at[target], returned.at[z], back_send.at[d], back_recv.at[d], {"batch": target}
        )

    def row_copy(d, i):
        target = lax.rem(x + d, mp)
        part = pl.ds(i * per_chunk, per_chunk)
        return remote(
            rows_hbm.at[part], raw.at[x, part], row_send.at[d, i], row_recv.at[d, i], {"mp": target}
        )

    def swap(n):
        return remote(
            weight_hbm.at[:, columns(other, n)],
            weights.at[z, c, n],
            swap_send.at[n],
            swap_recv.at[n],
            {"section": other},
        )

    def first_hop(direction, n):
        return remote(
            weight_hbm.at[:, columns(cross, n)],
            weights.at[z, c, n],
            line_send.at[direction, 0, n],
            line_recv.at[direction, 0, n],
            {"batch": z + (1 if direction == 0 else -1), "section": cross},
        )

    def later_hop(direction, hop, n, piece):
        return remote(
            weights.at[piece, cross, n],
            weights.at[piece, cross, n],
            line_send.at[direction, hop, n],
            line_recv.at[direction, hop, n],
            {"batch": z + (1 if direction == 0 else -1)},
        )

    def twin_copy(piece, n, kind):
        return remote(
            weights.at[piece, kind, n],
            weights.at[piece, kind, n],
            twin_send.at[piece, n],
            twin_recv.at[piece, n],
            {"group": twin},
        )

    def norm_copy(i):
        part = pl.ds(i * per_chunk, per_chunk)
        return remote(
            normed.at[c, :, part],
            normed.at[c, :, part],
            norm_send.at[i],
            norm_recv.at[i],
            {"section": other},
        )

    def sum_copy(d, e):
        peer, side = lax.rem(x + d, mp), lax.rem(c + e, 2)
        return remote(
            partial.at[side],
            logits_in.at[d * 2 + e],
            sum_send.at[d * 2 + e],
            sum_recv.at[d * 2 + e],
            {"mp": peer, "section": side},
        )

    own_copies = [
        pltpu.make_async_copy(keys_hbm.at[0], keys, local_sem.at[0]),
        pltpu.make_async_copy(values_hbm.at[0], values, local_sem.at[1]),
        pltpu.make_async_copy(mail_ref.at[z], mail_in.at[z], local_sem.at[2]),
        pltpu.make_async_copy(rows_hbm, raw.at[x], local_sem.at[3]),
    ]
    own_weights = [
        pltpu.make_async_copy(weight_hbm.at[:, columns(c, n)], weights.at[z, c, n], local_sem.at[5 + n])
        for n in range(chunks)
    ]

    for d in range(1, nb):
        mail(d).start()
    for n in range(chunks):

        @pl.when(z < nb - 1)
        def _():
            first_hop(0, n).start()

        @pl.when(z > 0)
        def _():
            first_hop(1, n).start()

    for i in range(row_chunks):
        for d in range(1, mp):
            row_copy(d, i).start()
    for copy in own_copies:
        copy.start()
    for n in range(chunks):
        swap(n).start()
    for copy in own_weights:
        copy.start()

    for side in range(2):
        total[side] = jnp.broadcast_to(
            bias_ref[:, pl.ds(pl.multiple_of(c * half, half), half)], total.shape[1:]
        )

    for copy in own_copies[:3]:
        copy.wait()
    for d in range(1, nb):
        mail(d).wait_recv()

    scale = 1.0 / HD**0.5
    context = page_count * keys.shape[1]
    head_of_row = lax.broadcasted_iota(jnp.int32, (heads, HD), 0) // group
    position = lax.broadcasted_iota(jnp.int32, (heads, context), 1)
    step = 4 if cap % 4 == 0 else cap
    blocks = cap // step

    def serve(d, r):
        base = (d * cap + r) * (page_count + 1)
        pages = [table_ref[base + i] for i in range(page_count)]
        length = table_ref[base + page_count]
        key_block = jnp.concatenate([keys[p] for p in pages], axis=0)
        value_block = jnp.concatenate([values[p] for p in pages], axis=0)
        letter = mail_in[d, r]
        query = letter[:heads]
        own_key = letter[heads : heads + kvl].astype(jnp.float32)
        own_value = letter[heads + kvl : heads + 2 * kvl].astype(jnp.float32)
        zero = jnp.zeros_like(query)
        wide = jnp.concatenate([jnp.where(head_of_row == h, query, zero) for h in range(kvl)], axis=1)
        scores = (
            lax.dot_general(
                wide, key_block, (((1,), (1,)), ((), ())), preferred_element_type=jnp.float32
            )
            * scale
        )
        scores = jnp.where(position < length, scores, -1e30)
        top = jnp.max(scores, axis=1, keepdims=True)
        w = jnp.exp(scores - top)
        den = jnp.sum(w, axis=1, keepdims=True)
        everything = jnp.dot(w.astype(jnp.bfloat16), value_block, preferred_element_type=jnp.float32)
        num = jnp.zeros((heads, HD), jnp.float32)
        key_rows = jnp.zeros((heads, HD), jnp.float32)
        value_rows = jnp.zeros((heads, HD), jnp.float32)
        for h in range(kvl):
            here = head_of_row == h
            num = jnp.where(here, everything[:, h * HD : (h + 1) * HD], num)
            key_rows = jnp.where(here, own_key[h : h + 1], key_rows)
            value_rows = jnp.where(here, own_value[h : h + 1], value_rows)
        own_score = jnp.sum(query.astype(jnp.float32) * key_rows, axis=1, keepdims=True) * scale
        own = jnp.exp(own_score - top)
        return ((num + own * value_rows) / (den + own)).astype(jnp.bfloat16)

    def serve_block(index, carry):
        d, r0 = index // blocks, lax.rem(index, blocks) * step
        results = [serve(d, r0 + u) for u in range(step)]
        for u in range(step):
            served_out[d, r0 + u] = results[u]
        return carry

    lax.fori_loop(0, nb * blocks, serve_block, 0)
    own_back = pltpu.make_async_copy(served_out.at[z], returned.at[z], local_sem.at[4])
    own_back.start()

    def line_step(r, n):
        @pl.when(z - r >= 0)
        def _():
            piece = z - r
            later_hop(0, r - 1, n, piece).wait_recv()

            @pl.when(z + 1 < nb)
            def _():
                later_hop(0, r, n, piece).start()

            twin_copy(piece, n, cross).start()

        @pl.when(z + r < nb)
        def _():
            piece = z + r
            later_hop(1, r - 1, n, piece).wait_recv()

            @pl.when(z > 0)
            def _():
                later_hop(1, r, n, piece).start()

            twin_copy(piece, n, cross).start()

    features = row_width * mp
    pieces_per_block = row_width // depth
    fine = min(16, per_chunk)

    def row_step(i):
        for d in range(1, mp):
            row_copy(d, i).wait_recv()

        def normalise(j, carry):
            start = pl.multiple_of(i * per_chunk + j * fine, fine)
            part = pl.ds(start, fine)
            power = jnp.zeros((fine, 1), jnp.float32)
            for b in range(mp):
                block = raw[b, part].astype(jnp.float32)
                power = power + jnp.sum(block * block, axis=1, keepdims=True)
            factor = lax.rsqrt(power / features + 1e-06)
            for b in range(mp):
                block = raw[b, part].astype(jnp.float32)
                gain = gain_ref[:, b * row_width : (b + 1) * row_width]
                result = (block * factor * gain).astype(jnp.bfloat16)
                for p in range(pieces_per_block):
                    normed[c, b * pieces_per_block + p, part] = result[:, p * depth : (p + 1) * depth]
            return carry

        lax.fori_loop(0, per_chunk // fine, normalise, 0)
        norm_copy(i).start()

    own_copies[3].wait()
    early = [(r, n) for r in range(1, nb - 1) for n in range(chunks)]
    for i in range(row_chunks):
        for r, n in early[len(early) * i // row_chunks : len(early) * (i + 1) // row_chunks]:
            line_step(r, n)
        row_step(i)
    for i in range(row_chunks):
        norm_copy(i).wait_recv()

    def multiply(piece, kind, n):
        for side in range(2):
            total[side, :, n * chunk : (n + 1) * chunk] += jnp.dot(
                normed[side, piece * ns + kind], weights[piece, kind, n], preferred_element_type=jnp.float32
            )

    def multiply_own(n):
        own_weights[n].wait()
        swap(n).wait_recv()
        multiply(z, 0, n)
        multiply(z, 1, n)

    def multiply_at(r, n):
        def both(piece):
            multiply(piece, cross, n)
            twin_copy(piece, n, 1 - cross).wait_recv()
            multiply(piece, 1 - cross, n)

        def left():
            both(z - r)

        def right():
            both(z + r)

        pl.when(z - r >= 0)(left)
        pl.when(z + r < nb)(right)

    for n in range(chunks):
        multiply_own(n)

        def near(r, carry):
            multiply_at(r, n)
            return carry

        lax.fori_loop(1, nb - 1, near, 0)
        line_step(nb - 1, n)
        if n == 0:
            for d in range(1, nb):
                back(d).start()

    for n in range(chunks):
        multiply_at(nb - 1, n)

    class_part = class_ref[:, pl.ds(pl.multiple_of(c * half, half), half)]
    for side in range(2):
        hidden = jnp.maximum(total[side], 0.0).astype(jnp.bfloat16)
        partial[side] = lax.dot_general(
            class_part, hidden, (((1,), (1,)), ((), ())), preferred_element_type=jnp.float32
        )
    pairs = [(d, e) for d in range(mp) for e in range(2) if d or e]
    for d, e in pairs:
        sum_copy(d, e).start()

    own_back.wait()
    for d in range(1, nb):
        back(d).wait_recv()
    pick = nb * cap * (page_count + 1)

    def place(j, carry):
        attention_ref[j] = returned[table_ref[pick + j], table_ref[pick + slots + j]]
        return carry

    lax.fori_loop(0, slots, place, 0)

    logits = partial[c]
    for d, e in pairs:
        sum_copy(d, e).wait_recv()
        logits = logits + logits_in[d * 2 + e]
    odds_ref[...] = (logits[1:2] + class_bias_ref[1]) - (logits[0:1] + class_bias_ref[0])

    for d in range(1, nb):
        mail(d).wait_send()
        back(d).wait_send()
    for i in range(row_chunks):
        for d in range(1, mp):
            row_copy(d, i).wait_send()
        norm_copy(i).wait_send()
    for d, e in pairs:
        sum_copy(d, e).wait_send()
    for n in range(chunks):
        swap(n).wait_send()

        @pl.when(z < nb - 1)
        def _():
            first_hop(0, n).wait_send()

        @pl.when(z > 0)
        def _():
            first_hop(1, n).wait_send()

        def drain(r, carry):
            @pl.when(z - r >= 0)
            def _():
                @pl.when(z + 1 < nb)
                def _():
                    later_hop(0, r, n, z - r).wait_send()

                twin_copy(z - r, n, cross).wait_send()

            @pl.when(z + r < nb)
            def _():
                @pl.when(z > 0)
                def _():
                    later_hop(1, r, n, z + r).wait_send()

                twin_copy(z + r, n, cross).wait_send()

            return carry

        lax.fori_loop(1, nb, drain, 0)


def per_device(
    queries,
    new_keys,
    new_values,
    key_pages,
    value_pages,
    page_table,
    ancestry,
    lengths,
    step_rows,
    norm_gain,
    head_weight,
    head_bias,
    class_weight,
    class_bias,
):
    slot_count, page_count = page_table.shape
    kv_width = key_pages.shape[3]
    kvl = kv_width // HD
    group = queries.shape[2] // kv_width
    heads = kvl * group
    nb, ng = lax.axis_size("batch"), lax.axis_size("group")
    mp, ns = lax.axis_size("mp"), lax.axis_size("section")
    assert ng == 2 and ns == 2 and queries.shape[0] == 1
    z = lax.axis_index("batch")
    cap = max(2, (2 * slot_count + nb - 1) // nb)

    source = (ancestry // slot_count).reshape(nb, slot_count)
    positions = jnp.arange(slot_count)
    earlier = positions[None, :] < positions[:, None]
    same_source = source[:, :, None] == source[:, None, :]
    rank = jnp.sum(same_source & earlier[None, :, :], axis=2)
    slot_ids = jnp.arange(cap)
    served = (source == z)[:, None, :] & (rank[:, None, :] == slot_ids[None, :, None])
    served_slot = jnp.sum(jnp.where(served, positions[None, None, :], 0), axis=2)
    own_source = lax.dynamic_index_in_dim(source, z, 0, keepdims=False)
    own_rank = lax.dynamic_index_in_dim(rank, z, 0, keepdims=False)
    local_lengths = lax.dynamic_slice_in_dim(lengths, z * slot_count, slot_count)
    facts = jnp.concatenate([page_table, local_lengths[:, None]], axis=1)
    table = jnp.concatenate([facts[served_slot].reshape(-1), own_source, own_rank])
    wanted = (own_source[None, None, :] == jnp.arange(nb)[:, None, None]) & (
        own_rank[None, None, :] == slot_ids[None, :, None]
    )
    request_slot = jnp.sum(jnp.where(wanted, positions[None, None, :], 0), axis=2)
    letters = jnp.concatenate([queries[0], new_keys[0], new_values[0]], axis=1)
    lines = heads + 2 * kvl
    mail = jnp.take(letters, request_slot.reshape(-1), axis=0).reshape(nb, cap, lines, HD)

    row_count, row_width = step_rows.shape
    depth, width = head_weight.shape
    half = width // ns
    chunk = min(256, half)
    chunks = half // chunk
    row_chunks = 4
    pieces = nb * ns
    dims = dict(
        nb=nb, ng=ng, mp=mp, ns=ns, cap=cap, page_count=page_count, kvl=kvl, group=group,
        half=half, chunk=chunk, chunks=chunks, depth=depth, row_chunks=row_chunks,
    )
    class_rows = jnp.zeros((8, width), class_weight.dtype).at[:2].set(class_weight.T)
    smem = pl.BlockSpec(memory_space=pltpu.SMEM)
    vmem = pl.BlockSpec(memory_space=pltpu.VMEM)
    anywhere = pl.BlockSpec(memory_space=pl.ANY)
    bf16, f32 = jnp.bfloat16, jnp.float32
    sems = pltpu.SemaphoreType.DMA
    attention, odds = pl.pallas_call(
        functools.partial(fused_kernel, dims),
        out_shape=(
            jax.ShapeDtypeStruct((slot_count, heads, HD), bf16),
            jax.ShapeDtypeStruct((1, row_count), f32),
        ),
        in_specs=[smem, smem, vmem, anywhere, anywhere, anywhere, vmem, anywhere, vmem, vmem],
        out_specs=(vmem, vmem),
        scratch_shapes=[
            pltpu.VMEM((nb, cap, lines, HD), bf16),
            pltpu.VMEM((nb, cap, heads, HD), bf16),
            pltpu.VMEM((nb, cap, heads, HD), bf16),
            pltpu.VMEM(key_pages.shape[1:], bf16),
            pltpu.VMEM(key_pages.shape[1:], bf16),
            pltpu.VMEM((mp, row_count, row_width), bf16),
            pltpu.VMEM((2, pieces, row_count, depth), bf16),
            pltpu.VMEM((nb, ns, chunks, depth, chunk), bf16),
            pltpu.VMEM((2, row_count, half), f32),
            pltpu.VMEM((2, 8, row_count), f32),
            pltpu.VMEM((2 * mp, 8, row_count), f32),
            sems((5 + chunks,)),
            sems((nb,)),
            sems((nb,)),
            sems((nb,)),
            sems((nb,)),
            sems((2, nb, chunks)),
            sems((2, nb, chunks)),
            sems((nb, chunks)),
            sems((nb, chunks)),
            sems((chunks,)),
            sems((chunks,)),
            sems((mp, row_chunks)),
            sems((mp, row_chunks)),
            sems((row_chunks,)),
            sems((row_chunks,)),
            sems((2 * mp,)),
            sems((2 * mp,)),
        ],
        compiler_params=pltpu.CompilerParams(
            collective_id=0, has_side_effects=True, vmem_limit_bytes=60 * 1024 * 1024
        ),
        name="filter_round",
    )(
        table,
        class_bias,
        mail,
        key_pages,
        value_pages,
        step_rows,
        norm_gain.reshape(1, -1),
        head_weight,
        head_bias.reshape(1, -1),
        class_rows,
    )
    return attention.reshape(1, slot_count, heads * HD), odds.reshape(-1)


def solution(mesh):
    placed = (
        P("section", ("group", "batch"), "mp"),
        P("section", ("group", "batch"), "mp"),
        P("section", ("group", "batch"), "mp"),
        P("section", ("group", "batch"), None, "mp"),
        P("section", ("group", "batch"), None, "mp"),
        P(("group", "batch"), None),
        P("group"),
        P("group"),
        P(("group", "batch", "section"), "mp"),
        P(),
        P(("batch", "section"), "mp"),
        P("mp"),
        P("mp", None),
        P(),
    )
    return jax.shard_map(
        per_device,
        mesh=mesh,
        in_specs=placed,
        out_specs=(P("section", ("group", "batch"), "mp"), P(("group", "batch", "section"))),
        check_vma=False,
    )
```
